32 devices in a mesh: sec: 2 (over core), elem: 16 (over z, y, x).
Axes of the slice: x: 2, y: 2, z: 4, core: 2. Of those that a mesh axis runs over, the one named last changes fastest.
Arguments:
- fields: float32 [2, 320, 16384], P('sec', None, 'elem'), may hold values from -6 to 6
- jacobian: float32 [2, 16384], P('sec', 'elem'), may hold values from 0.25 to 2.5
- face_links: int32 [2, 6, 16384], P('sec', None, 'elem'), may hold values from 0 to 1535, as said below
- volume_matrix: float32 [2, 320, 320], P('sec'), may hold values from -0.3125 to 0.3125
- face_matrices: float32 [2, 6, 320, 320], P('sec'), may hold values from -0.3125 to 0.3125
- patterns: float32 [4, 64, 64], replicated, may hold values from 0 to 0.03125
- donor_index: int32 [2, 2048], P('sec', 'elem'), may hold values from 0 to 1023
- pattern_index: int32 [2, 2048], P('sec', 'elem'), may hold values from 0 to 3
- receivers: int32 [2, 2048], P('sec', 'elem'), may hold values from -1 to 1023, as said below
Outputs:
- advanced: float32 [2, 320, 16384], P('sec', None, 'elem')
The draws below stay inside these ranges and needn't reach their ends.
Inputs may be any that keep to these rules, and one draw needn't show every extreme that they name: face_links[s, f, g] counts from the lowest rim element of the device holding element g; index 256 is that device's first own element. receivers holds on each device 8 slots for each device of the other section, source-major; -1 marks an empty slot, other entries on one device are distinct; in every draw some device gets 8 blocks from every device of the other section.
All inputs are finite; a program needn't handle non-finite values.
Results may differ from the reference program's by a relative error of at most 0.0001.
Values sent between devices are 32-bit elements; how exact they have to be, the bound alone decides.
A program may use at most 64 MiB of HBM per device.

```python
import math
import jax
import jax.numpy as jnp
from jax import lax

VARS = 5
NODES = 64
E_DEV = 1024
HALO = 256
CAP = 8
NPAT = 4
COMPONENTS = 320
NE = 16384
SLOTS = 128
TOTAL_SLOTS = 2048
N_ELEM = 16


def draw_face_links(key, part):
    subkeys = jax.random.split(jax.random.fold_in(key, 7), 3)
    grid_shape = (2, 6, NE)
    position = jnp.arange(NE, dtype=jnp.int32) % E_DEV
    near_reach = min(16, HALO)
    short_reach = jax.random.randint(subkeys[0], grid_shape, 1, near_reach + 1, dtype=jnp.int32)
    medium = jax.random.randint(subkeys[1], grid_shape, 1, HALO // 2 + 1, dtype=jnp.int32)
    far_reach = jax.random.randint(subkeys[2], grid_shape, HALO // 2, HALO + 1, dtype=jnp.int32)
    distance = jnp.concatenate([short_reach[:, 0:2], medium[:, 2:4], far_reach[:, 4:6]], axis=1)
    direction = jnp.array([-1, 1, -1, 1, -1, 1], jnp.int32)[None, :, None]
    neighbours = position[None, None, :] + HALO + direction * distance
    face_ids = jnp.arange(6, dtype=jnp.int32)[None, :, None]
    neighbours = jnp.where((face_ids == 4) & (position == 0)[None, None, :], 0, neighbours)
    neighbours = jnp.where((face_ids == 5) & (position == E_DEV - 1)[None, None, :], E_DEV + 2 * HALO - 1, neighbours)
    return neighbours.astype(jnp.int32)


def draw_receivers(key, part):
    sections = []
    for section in range(2):
        subkeys = jax.random.split(jax.random.fold_in(key, 11 + section), 3)
        counts = jax.random.randint(subkeys[0], (N_ELEM, N_ELEM), CAP // 2, CAP + 1, dtype=jnp.int32)
        source = jnp.arange(N_ELEM, dtype=jnp.int32)[:, None]
        target = jnp.arange(N_ELEM, dtype=jnp.int32)[None, :]
        quarter = N_ELEM // 4
        reach = 3 * N_ELEM // 4
        if section == 1:
            banded = (target - source // quarter * quarter) % N_ELEM < reach
        else:
            banded = (source - target // quarter * quarter) % N_ELEM < reach
        busiest = jax.random.randint(subkeys[1], (), 0, N_ELEM, dtype=jnp.int32)
        counts = jnp.where(target == busiest, CAP, jnp.where(banded, counts, 0))
        orders = jax.vmap(lambda subkey: jax.random.permutation(subkey, E_DEV))(jax.random.split(subkeys[2], N_ELEM)).astype(jnp.int32)
        leading = orders[:, :1]
        orders = jnp.where(orders == E_DEV - 1, leading, orders)
        orders = orders.at[:, 0].set(E_DEV - 1)
        slot_number = jnp.arange(N_ELEM * CAP, dtype=jnp.int32)
        sender = slot_number // CAP
        within = slot_number % CAP
        limit = jnp.transpose(counts)[:, sender]
        values = jnp.where(within[None, :] < limit, orders[:, :N_ELEM * CAP], -1)
        sections.append(values.reshape(-1))
    return jnp.stack(sections).astype(jnp.int32)


def set_ends(values, key, smallest, top_value):
    shape = values.shape
    spot = [jax.random.randint(jax.random.fold_in(key, axis), (), 0, shape[axis]) for axis in range(len(shape))]
    values = values.at[tuple(spot)].set(smallest)
    longest = shape.index(max(shape))
    spot[longest] = (spot[longest] + 1) % shape[longest]
    return values.at[tuple(spot)].set(top_value)


def levels(key, extent, pieces, smallest, top_value):
    def one(dim, blocks):
        draws = jax.random.uniform(jax.random.fold_in(jax.random.fold_in(key, 6), dim), (blocks,), jnp.float32, smallest / len(pieces), top_value / len(pieces))
        return jnp.repeat(jnp.exp(draws), extent[dim] // blocks).reshape((-1,) + (1,) * (len(extent) - dim - 1))

    gain = one(*pieces[0])
    for cut in pieces[1:]:
        gain = gain * one(*cut)
    return gain


def noise(key, dims, spread, bound, cuts=(), kind=jnp.bfloat16):
    drawn = jax.random.normal(key, dims, jnp.float32) * spread
    if len(cuts) > 0:
        drawn = levels(key, dims, cuts, -0.22, 0.18) * drawn
    return jnp.clip(drawn, min=-bound, max=bound).astype(kind)


def setup_inputs(seed: int = 0) -> dict:
    seeds = jax.random.split(jax.random.key(seed), 10)
    return {
        "fields": noise(seeds[0], (2, COMPONENTS, NE), 1.0, 6.0, ((0, 2), (2, 16)), jnp.float32),
        "jacobian": jnp.clip(jnp.exp(math.log(2.5) - 2.3025851 * jax.random.uniform(seeds[1], (2, NE), jnp.float32) ** levels(seeds[1], (2, NE), ((0, 2), (1, 16)), -0.2, 0.2)), 0.25, 2.5),
        "face_links": draw_face_links(jax.random.fold_in(seeds[9], 71), 0),
        "volume_matrix": noise(seeds[3], (2, COMPONENTS, COMPONENTS), COMPONENTS ** -0.5, 0.3125, ((0, 2),), jnp.float32),
        "face_matrices": noise(seeds[4], (2, 6, COMPONENTS, COMPONENTS), COMPONENTS ** -0.5, 0.3125, ((0, 2),), jnp.float32),
        "patterns": jnp.clip(jax.random.uniform(seeds[5], (NPAT, NODES, NODES), jnp.float32, 0.0, 0.03125), 0.0, 0.03125),
        "donor_index": set_ends(jax.random.randint(seeds[6], (2, TOTAL_SLOTS), 0, E_DEV), jax.random.fold_in(seeds[6], 1), 0, E_DEV - 1).astype(jnp.int32),
        "pattern_index": set_ends(jax.random.randint(seeds[7], (2, TOTAL_SLOTS), 0, NPAT), jax.random.fold_in(seeds[7], 1), 0, NPAT - 1).astype(jnp.int32),
        "receivers": draw_receivers(jax.random.fold_in(seeds[9], 71), 0),
    }


time_step = 0.25


def section_rate(values, inverse_volume, neighbours, volume_block, face_blocks):
    padded = jnp.pad(values, ((0, 0), (HALO, HALO)))
    element = jnp.arange(NE, dtype=jnp.int32)
    anchor = (element // E_DEV) * E_DEV
    summed = jnp.dot(volume_block, values, precision=lax.Precision.HIGHEST, preferred_element_type=jnp.float32)
    for direction in range(6):
        column = (anchor + neighbours[direction]).astype(jnp.int32)
        summed = summed + jnp.dot(face_blocks[direction], jnp.take(padded, column, axis=1), precision=lax.Precision.HIGHEST, preferred_element_type=jnp.float32)
    return inverse_volume[None, :] * summed


def interpolate(values, donors, choose, patterns):
    columns = jnp.take(values, donors, axis=1).reshape(VARS, NODES, -1)
    result = jnp.zeros_like(columns)
    for which_one in range(NPAT):
        mapped = jnp.einsum("mn,vnc->vmc", patterns[which_one], columns, precision=lax.Precision.HIGHEST)
        result = jnp.where(choose[None, None, :] == which_one, mapped, result)
    return result.reshape(VARS * NODES, -1)


def fringe(fields, donor_index, pattern_index, receivers, patterns):
    slot_owner = jnp.arange(TOTAL_SLOTS, dtype=jnp.int32) // SLOTS
    blocks = []
    for section in range(2):
        donors = (slot_owner * E_DEV + donor_index[section]).astype(jnp.int32)
        blocks.append(interpolate(fields[section], donors, pattern_index[section], patterns))
    updated = []
    for section in range(2):
        source = blocks[1 - section].reshape(VARS * NODES, N_ELEM, N_ELEM, CAP)
        source = jnp.transpose(source, (0, 2, 1, 3)).reshape(VARS * NODES, TOTAL_SLOTS)
        target = receivers[section]
        place = jnp.where(target >= 0, slot_owner * E_DEV + target, NE).astype(jnp.int32)
        updated.append(fields[section].at[:, place].set(source, mode="drop"))
    return jnp.stack(updated)


def rate(values, jacobian, face_links, volume_matrix, face_matrices):
    return jnp.stack([section_rate(values[section], jacobian[section], face_links[section], volume_matrix[section], face_matrices[section]) for section in range(2)])


def reference(fields, jacobian, face_links, volume_matrix, face_matrices, patterns, donor_index, pattern_index, receivers):
    first_segment = fringe(fields, donor_index, pattern_index, receivers, patterns)
    middle = first_segment + time_step * rate(first_segment, jacobian, face_links, volume_matrix, face_matrices)
    second = fringe(middle, donor_index, pattern_index, receivers, patterns)
    return 0.5 * first_segment + 0.5 * (second + time_step * rate(second, jacobian, face_links, volume_matrix, face_matrices))
```

```python
import functools

import jax
import jax.numpy as jnp
from jax import lax
from jax.experimental import pallas as pl
from jax.experimental.pallas import tpu as pltpu
from jax.sharding import PartitionSpec as P

NODES = 64
HALO = 256
LANES = 128
ROWS = 4
DEPTH = 384
PARTS = DEPTH // LANES
STEP = 0.25
MESH = pl.DeviceIdType.MESH
F32 = jnp.float32
BF16 = jnp.bfloat16


def split(value):
    high = value.astype(BF16)
    return high, (value - high.astype(F32)).astype(BF16)


def kernel(
    n,
    links,
    scale,
    donors,
    select,
    fields,
    volume,
    faces,
    patterns,
    choose,
    out,
    table,
    landed,
    first,
    second,
    donated,
    outgoing,
    packed,
    rims,
    operand,
    weights,
    padded,
    own,
    mapped,
    block_send,
    block_recv,
    rim_send,
    rim_recv,
):
    sec, me = lax.axis_index("sec"), lax.axis_index("elem")
    other = 1 - sec
    elements = fields.shape[1]
    slots = donors.shape[1]
    per_device = slots // n
    block = per_device * ROWS
    components = fields.shape[0]
    tail = components - 2 * LANES

    barrier = pltpu.get_barrier_semaphore()
    for j in range(n):
        pl.semaphore_signal(barrier, inc=1, device_id=(other, j), device_id_type=MESH)

    @pl.when(me > 0)
    def _():
        pl.semaphore_signal(barrier, inc=1, device_id=(sec, me - 1), device_id_type=MESH)

    @pl.when(me < n - 1)
    def _():
        pl.semaphore_signal(barrier, inc=1, device_id=(sec, me + 1), device_id_type=MESH)

    for c in range(elements // LANES):
        for j in range(PARTS):
            if j < 2:
                piece = fields[j * LANES : (j + 1) * LANES, c * LANES : (c + 1) * LANES]
            else:
                piece = jnp.concatenate(
                    [
                        fields[2 * LANES : components, c * LANES : (c + 1) * LANES],
                        jnp.zeros((LANES - tail, LANES), F32),
                    ],
                    axis=0,
                )
            table[pl.ds(c * LANES * ROWS + j, LANES, stride=ROWS), :] = jnp.transpose(piece)
        table[pl.ds(c * LANES * ROWS + 3, LANES, stride=ROWS), :] = jnp.zeros((LANES, LANES), F32)

    def prepare_weights():
        padded[...] = jnp.zeros_like(padded)
        for f in range(7):
            padded[0:components, 0:components] = volume[...] if f == 6 else faces[f]
            for k in range(PARTS):
                strip = jnp.transpose(padded[:, k * LANES : (k + 1) * LANES])
                high, low = split(strip)
                weights[f, k * LANES : (k + 1) * LANES, :] = high
                weights[f, DEPTH + k * LANES : DEPTH + (k + 1) * LANES, :] = high
                weights[f, 2 * DEPTH + k * LANES : 2 * DEPTH + (k + 1) * LANES, :] = low

    def rim_copy(stage, side):
        target = me - 1 if side == 0 else me + 1
        return pltpu.make_async_remote_copy(
            src_ref=packed.at[side],
            dst_ref=rims.at[stage, 1 - side],
            send_sem=rim_send.at[stage, side],
            recv_sem=rim_recv.at[stage, 1 - side],
            device_id=(sec, target),
            device_id_type=MESH,
        )

    def to_operand(row, count, parts):
        for k in range(PARTS):
            high, low = split(parts[k])
            operand[pl.ds(row, count), k * LANES : (k + 1) * LANES] = high
            operand[pl.ds(row, count), DEPTH + k * LANES : DEPTH + (k + 1) * LANES] = low
            operand[pl.ds(row, count), 2 * DEPTH + k * LANES : 2 * DEPTH + (k + 1) * LANES] = high

    def face_products(row):
        def body(f, carry):
            y = jnp.dot(
                operand[pl.ds(pl.multiple_of(row, HALO), HALO), :],
                weights[f],
                preferred_element_type=F32,
            )
            for k in range(PARTS):
                mapped[f, pl.ds(row * ROWS + k, HALO, stride=ROWS), :] = y[:, k * LANES : (k + 1) * LANES]
            return carry

        lax.fori_loop(0, 6, body, 0)

    for stage in range(2):
        state = first if stage == 0 else second

        def donate(i, carry):
            for u in range(8):
                b = i * 8 + u
                row = donors[0, b] * ROWS
                donated[pl.ds(pl.multiple_of(b * ROWS, ROWS), ROWS), :] = table[pl.ds(row, ROWS), :]
            return carry

        lax.fori_loop(0, slots // 8, donate, 0)
        values = donated[...]
        kinds = choose[...]
        result = jnp.zeros((slots * ROWS, LANES), F32)
        for p in range(patterns.shape[0]):
            moved = jnp.dot(values, patterns[p], precision=lax.Precision.HIGHEST, preferred_element_type=F32)
            result = jnp.where(kinds == p, moved, result)
        outgoing[...] = result

        if stage == 0:
            heard = n + (me > 0).astype(jnp.int32) + (me < n - 1).astype(jnp.int32)
            pl.semaphore_wait(barrier, heard)

        def block_copy(j):
            return pltpu.make_async_remote_copy(
                src_ref=outgoing.at[pl.ds(pl.multiple_of(j * block, block), block)],
                dst_ref=landed.at[stage, pl.ds(pl.multiple_of(me * block, block), block)],
                send_sem=block_send.at[stage, j],
                recv_sem=block_recv.at[stage, me],
                device_id=(other, j),
                device_id_type=MESH,
            )

        def arrived(j):
            return pltpu.make_async_remote_copy(
                src_ref=outgoing.at[pl.ds(pl.multiple_of(j * block, block), block)],
                dst_ref=landed.at[stage, pl.ds(pl.multiple_of(j * block, block), block)],
                send_sem=block_send.at[stage, j],
                recv_sem=block_recv.at[stage, j],
                device_id=(other, j),
                device_id_type=MESH,
            )

        for j in range(n):
            block_copy(j).start()
        if stage == 0:
            prepare_weights()
        for j in range(n):
            arrived(j).wait_recv()
        table[elements * ROWS :, :] = landed[stage]

        def pick(i, carry):
            for u in range(8):
                g = i * 8 + u
                row = select[0, g] * ROWS
                state[pl.ds(pl.multiple_of(g * ROWS, ROWS), ROWS), :] = table[pl.ds(row, ROWS), :]
            return carry

        def rim_parts(row):
            return [state[pl.ds(row * ROWS + k, HALO, stride=ROWS), :] for k in range(PARTS)]

        for side, begin in ((0, 0), (1, elements - HALO)):
            lax.fori_loop(begin // 8, (begin + HALO) // 8, pick, 0)
            parts = rim_parts(begin)
            packed[side, 0:HALO, :] = parts[0]
            packed[side, HALO : 2 * HALO, :] = parts[1]
            lower, upper = parts[2][: HALO // 2], parts[2][HALO // 2 :]
            packed[side, 2 * HALO :, :] = lower + pltpu.roll(upper, tail, 1)

            @pl.when(me > 0 if side == 0 else me < n - 1)
            def _():
                rim_copy(stage, side).start()

            to_operand(HALO + begin, HALO, parts)
        lax.fori_loop(HALO // 8, (elements - HALO) // 8, pick, 0)
        for c in range(1, elements // HALO - 1):
            to_operand(HALO + c * HALO, HALO, rim_parts(c * HALO))

        def own_products(c, carry):
            row = HALO + c * HALO
            face_products(row)
            y = jnp.dot(
                operand[pl.ds(pl.multiple_of(row, HALO), HALO), :],
                weights[6],
                preferred_element_type=F32,
            )
            for k in range(PARTS):
                own[pl.ds(c * HALO * ROWS + k, HALO, stride=ROWS), :] = y[:, k * LANES : (k + 1) * LANES]
            return carry

        lax.fori_loop(0, elements // HALO, own_products, 0)

        for side in range(2):
            row = 0 if side == 0 else HALO + elements
            inside = me > 0 if side == 0 else me < n - 1

            @pl.when(inside)
            def _():
                rim_copy(stage, 1 - side).wait_recv()
                folded = rims[stage, side, 2 * HALO :, :]
                lane = lax.broadcasted_iota(jnp.int32, folded.shape, 1)
                lower = jnp.where(lane < tail, folded, 0.0)
                upper = jnp.where(lane < tail, pltpu.roll(folded, LANES - tail, 1), 0.0)
                last = jnp.concatenate([lower, upper], axis=0)
                to_operand(row, HALO, [rims[stage, side, 0:HALO, :], rims[stage, side, HALO : 2 * HALO, :], last])
                face_products(row)

            @pl.when(jnp.logical_not(inside))
            def _():
                for f in range(6):
                    mapped[f, row * ROWS : (row + HALO) * ROWS, :] = jnp.zeros((HALO * ROWS, LANES), F32)

        def advance(i, carry):
            for u in range(8):
                g = i * 8 + u
                here = pl.ds(pl.multiple_of(g * ROWS, ROWS), ROWS)
                total = own[here, :]
                for f in range(6):
                    row = links[f, g] * ROWS
                    total = total + mapped[f, pl.ds(row, ROWS), :]
                stepped = state[here, :] + (STEP * scale[0, g]) * total
                if stage == 0:
                    table[here, :] = stepped
                else:
                    table[here, :] = 0.5 * first[here, :] + 0.5 * stepped
            return carry

        lax.fori_loop(0, elements // 8, advance, 0)
        for j in range(n):
            block_copy(j).wait_send()
        for side in range(2):

            @pl.when(me > 0 if side == 0 else me < n - 1)
            def _():
                rim_copy(stage, side).wait_send()

    for c in range(elements // LANES):
        for j in range(PARTS):
            piece = jnp.transpose(table[pl.ds(c * LANES * ROWS + j, LANES, stride=ROWS), :])
            high = min((j + 1) * LANES, components)
            out[j * LANES : high, c * LANES : (c + 1) * LANES] = piece[: high - j * LANES]


def local(
    n,
    fields,
    jacobian,
    face_links,
    volume_matrix,
    face_matrices,
    patterns,
    donor_index,
    pattern_index,
    receivers,
):
    components, elements = fields.shape[1:]
    slots = donor_index.shape[1]
    slot = jnp.arange(slots, dtype=jnp.int32)
    hit = receivers[0][None, :] == jnp.arange(elements, dtype=jnp.int32)[:, None]
    found = jnp.max(jnp.where(hit, slot[None, :], -1), axis=1)
    index = jnp.arange(elements, dtype=jnp.int32)
    select = jnp.where(found >= 0, elements + found, index)[None]
    choose = jnp.broadcast_to(
        jnp.repeat(pattern_index[0], ROWS)[:, None], (slots * ROWS, LANES)
    )
    turned = jnp.transpose(patterns, (0, 2, 1))
    empty = jnp.zeros_like(turned)
    twice = jnp.concatenate(
        [jnp.concatenate([turned, empty], axis=2), jnp.concatenate([empty, turned], axis=2)], axis=1
    )
    smem = pl.BlockSpec(memory_space=pltpu.SMEM)
    vmem = pl.BlockSpec(memory_space=pltpu.VMEM)
    wide = elements + 2 * HALO
    result = pl.pallas_call(
        functools.partial(kernel, n),
        out_shape=jax.ShapeDtypeStruct((components, elements), F32),
        in_specs=[smem] * 4 + [vmem] * 5,
        out_specs=vmem,
        scratch_shapes=[
            pltpu.VMEM(((elements + slots) * ROWS, LANES), F32),
            pltpu.VMEM((2, slots * ROWS, LANES), F32),
            pltpu.VMEM((elements * ROWS, LANES), F32),
            pltpu.VMEM((elements * ROWS, LANES), F32),
            pltpu.VMEM((slots * ROWS, LANES), F32),
            pltpu.VMEM((slots * ROWS, LANES), F32),
            pltpu.VMEM((2, 5 * HALO // 2, LANES), F32),
            pltpu.VMEM((2, 2, 5 * HALO // 2, LANES), F32),
            pltpu.VMEM((wide, 3 * DEPTH), BF16),
            pltpu.VMEM((7, 3 * DEPTH, DEPTH), BF16),
            pltpu.VMEM((DEPTH, DEPTH), F32),
            pltpu.VMEM((elements * ROWS, LANES), F32),
            pltpu.VMEM((6, wide * ROWS, LANES), F32),
            pltpu.SemaphoreType.DMA((2, n)),
            pltpu.SemaphoreType.DMA((2, n)),
            pltpu.SemaphoreType.DMA((2, 2)),
            pltpu.SemaphoreType.DMA((2, 2)),
        ],
        compiler_params=pltpu.CompilerParams(
            collective_id=0, has_side_effects=True, vmem_limit_bytes=62 * 1024 * 1024
        ),
    )(
        face_links[0],
        jacobian,
        donor_index,
        select,
        fields[0],
        volume_matrix[0],
        face_matrices[0],
        twice,
        choose,
    )
    return result[None]


def solution(mesh):
    return jax.shard_map(
        functools.partial(local, mesh.shape["elem"]),
        mesh=mesh,
        in_specs=(
            P("sec", None, "elem"),
            P("sec", "elem"),
            P("sec", None, "elem"),
            P("sec", None, None),
            P("sec", None, None, None),
            P(),
            P("sec", "elem"),
            P("sec", "elem"),
            P("sec", "elem"),
        ),
        out_specs=P("sec", None, "elem"),
        check_vma=False,
    )
```

```python
import functools

import jax
import jax.numpy as jnp
from jax import lax
from jax.experimental import pallas as pl
from jax.experimental.pallas import tpu as pltpu
from jax.sharding import PartitionSpec as P

NODES = 64
HALO = 256
LANES = 128
ROWS = 4
DEPTH = 384
PARTS = DEPTH // LANES
STEP = 0.25
MESH = pl.DeviceIdType.MESH
F32 = jnp.float32
BF16 = jnp.bfloat16


def split(value):
    high = value.astype(BF16)
    return high, (value - high.astype(F32)).astype(BF16)


def kernel(
    n,
    links,
    scale,
    donors,
    select,
    fields,
    volume,
    faces,
    patterns,
    choose,
    out,
    table,
    landed,
    first,
    second,
    donated,
    outgoing,
    packed,
    rims,
    operand,
    weights,
    padded,
    own,
    mapped,
    block_send,
    block_recv,
    rim_send,
    rim_recv,
):
    sec, me = lax.axis_index("sec"), lax.axis_index("elem")
    other = 1 - sec
    elements = fields.shape[1]
    slots = donors.shape[1]
    per_device = slots // n
    block = per_device * ROWS
    components = fields.shape[0]
    tail = components - 2 * LANES

    barrier = pltpu.get_barrier_semaphore()
    for j in range(n):
        pl.semaphore_signal(barrier, inc=1, device_id=(other, j), device_id_type=MESH)

    @pl.when(me > 0)
    def _():
        pl.semaphore_signal(barrier, inc=1, device_id=(sec, me - 1), device_id_type=MESH)

    @pl.when(me < n - 1)
    def _():
        pl.semaphore_signal(barrier, inc=1, device_id=(sec, me + 1), device_id_type=MESH)

    for c in range(elements // LANES):
        for j in range(PARTS):
            if j < 2:
                piece = fields[j * LANES : (j + 1) * LANES, c * LANES : (c + 1) * LANES]
            else:
                piece = jnp.concatenate(
                    [
                        fields[2 * LANES : components, c * LANES : (c + 1) * LANES],
                        jnp.zeros((LANES - tail, LANES), F32),
                    ],
                    axis=0,
                )
            table[pl.ds(c * LANES * ROWS + j, LANES, stride=ROWS), :] = jnp.transpose(piece)
        table[pl.ds(c * LANES * ROWS + 3, LANES, stride=ROWS), :] = jnp.zeros((LANES, LANES), F32)

    def prepare_weights():
        padded[...] = jnp.zeros_like(padded)
        for f in range(7):
            padded[0:components, 0:components] = volume[...] if f == 6 else faces[f]
            for k in range(PARTS):
                strip = jnp.transpose(padded[:, k * LANES : (k + 1) * LANES])
                high, low = split(strip)
                pair, lanes = f // 2, slice(f % 2 * DEPTH, f % 2 * DEPTH + DEPTH)
                if k < 2:
                    places = ((k * LANES, high), ((2 + k) * LANES, high), ((4 + k) * LANES, low))
                    for row, value in places:
                        weights[pair, row : row + LANES, lanes] = value
                else:
                    ends = (high[:tail], high[:tail], low[:tail], jnp.zeros_like(low[:tail]))
                    for m, value in enumerate(ends):
                        row = 6 * LANES + m * tail
                        weights[pair, row : row + tail, lanes] = value

    def rim_copy(stage, side):
        target = me - 1 if side == 0 else me + 1
        return pltpu.make_async_remote_copy(
            src_ref=packed.at[side],
            dst_ref=rims.at[stage, 1 - side],
            send_sem=rim_send.at[stage, side],
            recv_sem=rim_recv.at[stage, 1 - side],
            device_id=(sec, target),
            device_id_type=MESH,
        )

    def to_operand(row, count, parts):
        rows = pl.ds(row, count)
        for k in range(2):
            high, low = split(parts[k])
            operand[rows, k * LANES : (k + 1) * LANES] = high
            operand[rows, (2 + k) * LANES : (3 + k) * LANES] = low
            operand[rows, (4 + k) * LANES : (5 + k) * LANES] = high
        high, low = split(parts[2])
        both = high.astype(F32) + pltpu.roll(low.astype(F32), tail, 1)
        operand[rows, 6 * LANES : 7 * LANES] = both.astype(BF16)
        operand[rows, 7 * LANES : 8 * LANES] = high

    def face_products(row):
        def body(pair, carry):
            y = jnp.dot(
                operand[pl.ds(pl.multiple_of(row, HALO), HALO), :],
                weights[pair],
                preferred_element_type=F32,
            )
            for half in range(2):
                for k in range(PARTS):
                    at = half * DEPTH + k * LANES
                    mapped[pair * 2 + half, pl.ds(row * ROWS + k, HALO, stride=ROWS), :] = y[:, at : at + LANES]
            return carry

        lax.fori_loop(0, 3, body, 0)

    for stage in range(2):
        state = first if stage == 0 else second

        def donate(i, carry):
            for u in range(8):
                b = i * 8 + u
                row = donors[0, b] * ROWS
                donated[pl.ds(pl.multiple_of(b * ROWS, ROWS), ROWS), :] = table[pl.ds(row, ROWS), :]
            return carry

        lax.fori_loop(0, slots // 8, donate, 0)
        values = donated[...]
        shape = (slots * ROWS, slots)
        mine = lax.broadcasted_iota(jnp.int32, shape, 0) // ROWS == lax.broadcasted_iota(jnp.int32, shape, 1)
        kinds = jnp.sum(jnp.where(mine, choose[...].astype(F32), 0.0), axis=1, keepdims=True)
        result = jnp.zeros((slots * ROWS, LANES), F32)
        for p in range(patterns.shape[0]):
            one = patterns[p]
            none = jnp.zeros_like(one)
            twice = jnp.concatenate(
                [jnp.concatenate([one, none], axis=1), jnp.concatenate([none, one], axis=1)], axis=0
            )
            moved = lax.dot_general(
                values,
                twice,
                (((1,), (1,)), ((), ())),
                precision=lax.Precision.HIGHEST,
                preferred_element_type=F32,
            )
            result = jnp.where(kinds == float(p), moved, result)
        outgoing[...] = result

        if stage == 0:
            heard = n + (me > 0).astype(jnp.int32) + (me < n - 1).astype(jnp.int32)
            pl.semaphore_wait(barrier, heard)

        def block_copy(j):
            return pltpu.make_async_remote_copy(
                src_ref=outgoing.at[pl.ds(pl.multiple_of(j * block, block), block)],
                dst_ref=landed.at[stage, pl.ds(pl.multiple_of(me * block, block), block)],
                send_sem=block_send.at[stage, j],
                recv_sem=block_recv.at[stage, me],
                device_id=(other, j),
                device_id_type=MESH,
            )

        def arrived(j):
            return pltpu.make_async_remote_copy(
                src_ref=outgoing.at[pl.ds(pl.multiple_of(j * block, block), block)],
                dst_ref=landed.at[stage, pl.ds(pl.multiple_of(j * block, block), block)],
                send_sem=block_send.at[stage, j],
                recv_sem=block_recv.at[stage, j],
                device_id=(other, j),
                device_id_type=MESH,
            )

        for j in range(n):
            block_copy(j).start()
        if stage == 0:
            prepare_weights()
        for j in range(n):
            arrived(j).wait_recv()
        table[elements * ROWS :, :] = landed[stage]

        def pick(i, carry):
            for u in range(8):
                g = i * 8 + u
                row = select[0, g] * ROWS
                state[pl.ds(pl.multiple_of(g * ROWS, ROWS), ROWS), :] = table[pl.ds(row, ROWS), :]
            return carry

        def rim_parts(row):
            return [state[pl.ds(row * ROWS + k, HALO, stride=ROWS), :] for k in range(PARTS)]

        for side, begin in ((0, 0), (1, elements - HALO)):
            lax.fori_loop(begin // 8, (begin + HALO) // 8, pick, 0)
            parts = rim_parts(begin)
            packed[side, 0:HALO, :] = parts[0]
            packed[side, HALO : 2 * HALO, :] = parts[1]
            lower, upper = parts[2][: HALO // 2], parts[2][HALO // 2 :]
            packed[side, 2 * HALO :, :] = lower + pltpu.roll(upper, tail, 1)

            @pl.when(me > 0 if side == 0 else me < n - 1)
            def _():
                rim_copy(stage, side).start()

            to_operand(HALO + begin, HALO, parts)
        lax.fori_loop(HALO // 8, (elements - HALO) // 8, pick, 0)
        for c in range(1, elements // HALO - 1):
            to_operand(HALO + c * HALO, HALO, rim_parts(c * HALO))

        def own_products(c, carry):
            row = HALO + c * HALO
            face_products(row)
            y = jnp.dot(
                operand[pl.ds(pl.multiple_of(row, HALO), HALO), :],
                weights[3, :, 0:DEPTH],
                preferred_element_type=F32,
            )
            for k in range(PARTS):
                own[pl.ds(c * HALO * ROWS + k, HALO, stride=ROWS), :] = y[:, k * LANES : (k + 1) * LANES]
            return carry

        lax.fori_loop(0, elements // HALO, own_products, 0)

        for side in (1, 0):
            row = 0 if side == 0 else HALO + elements
            inside = me > 0 if side == 0 else me < n - 1

            @pl.when(inside)
            def _():
                rim_copy(stage, 1 - side).wait_recv()
                folded = rims[stage, side, 2 * HALO :, :]
                lane = lax.broadcasted_iota(jnp.int32, folded.shape, 1)
                lower = jnp.where(lane < tail, folded, 0.0)
                upper = jnp.where(lane < tail, pltpu.roll(folded, LANES - tail, 1), 0.0)
                last = jnp.concatenate([lower, upper], axis=0)
                to_operand(row, HALO, [rims[stage, side, 0:HALO, :], rims[stage, side, HALO : 2 * HALO, :], last])
                face_products(row)

            @pl.when(jnp.logical_not(inside))
            def _():
                for f in range(6):
                    mapped[f, row * ROWS : (row + HALO) * ROWS, :] = jnp.zeros((HALO * ROWS, LANES), F32)

        def advance(i, carry):
            for u in range(8):
                g = i * 8 + u
                here = pl.ds(pl.multiple_of(g * ROWS, ROWS), ROWS)
                total = own[here, :]
                for f in range(6):
                    row = links[f, 0, g] * ROWS
                    total = total + mapped[f, pl.ds(row, ROWS), :]
                stepped = state[here, :] + scale[0, g] * (STEP * total)
                if stage == 0:
                    table[here, :] = stepped
                else:
                    table[here, :] = 0.5 * first[here, :] + 0.5 * stepped
            return carry

        lax.fori_loop(0, elements // 8, advance, 0)
        for j in range(n):
            block_copy(j).wait_send()
        for side in range(2):

            @pl.when(me > 0 if side == 0 else me < n - 1)
            def _():
                rim_copy(stage, side).wait_send()

    for c in range(elements // LANES):
        for j in range(PARTS):
            piece = jnp.transpose(table[pl.ds(c * LANES * ROWS + j, LANES, stride=ROWS), :])
            high = min((j + 1) * LANES, components)
            out[j * LANES : high, c * LANES : (c + 1) * LANES] = piece[: high - j * LANES]


def local(
    n,
    fields,
    jacobian,
    face_links,
    volume_matrix,
    face_matrices,
    patterns,
    donor_index,
    pattern_index,
    receivers,
):
    components, elements = fields.shape[1:]
    slots = donor_index.shape[1]
    slot = jnp.arange(slots, dtype=jnp.int32)
    hit = receivers[0][None, :] == jnp.arange(elements, dtype=jnp.int32)[:, None]
    found = jnp.max(jnp.where(hit, slot[None, :], -1), axis=1)
    index = jnp.arange(elements, dtype=jnp.int32)
    select = jnp.where(found >= 0, elements + found, index)[None]
    smem = pl.BlockSpec(memory_space=pltpu.SMEM)
    vmem = pl.BlockSpec(memory_space=pltpu.VMEM)
    wide = elements + 2 * HALO
    result = pl.pallas_call(
        functools.partial(kernel, n),
        out_shape=jax.ShapeDtypeStruct((components, elements), F32),
        in_specs=[smem] * 4 + [vmem] * 5,
        out_specs=vmem,
        scratch_shapes=[
            pltpu.VMEM(((elements + slots) * ROWS, LANES), F32),
            pltpu.VMEM((2, slots * ROWS, LANES), F32),
            pltpu.VMEM((elements * ROWS, LANES), F32),
            pltpu.VMEM((elements * ROWS, LANES), F32),
            pltpu.VMEM((slots * ROWS, LANES), F32),
            pltpu.VMEM((slots * ROWS, LANES), F32),
            pltpu.VMEM((2, 5 * HALO // 2, LANES), F32),
            pltpu.VMEM((2, 2, 5 * HALO // 2, LANES), F32),
            pltpu.VMEM((wide, 8 * LANES), BF16),
            pltpu.VMEM((4, 8 * LANES, 2 * DEPTH), BF16),
            pltpu.VMEM((DEPTH, DEPTH), F32),
            pltpu.VMEM((elements * ROWS, LANES), F32),
            pltpu.VMEM((6, wide * ROWS, LANES), F32),
            pltpu.SemaphoreType.DMA((2, n)),
            pltpu.SemaphoreType.DMA((2, n)),
            pltpu.SemaphoreType.DMA((2, 2)),
            pltpu.SemaphoreType.DMA((2, 2)),
        ],
        compiler_params=pltpu.CompilerParams(
            collective_id=0, has_side_effects=True, vmem_limit_bytes=62 * 1024 * 1024
        ),
    )(
        jnp.transpose(face_links, (1, 0, 2)),
        jacobian,
        donor_index,
        select,
        fields[0],
        volume_matrix[0],
        face_matrices[0],
        patterns,
        pattern_index,
    )
    return result[None]


def solution(mesh):
    return jax.shard_map(
        functools.partial(local, mesh.shape["elem"]),
        mesh=mesh,
        in_specs=(
            P("sec", None, "elem"),
            P("sec", "elem"),
            P("sec", None, "elem"),
            P("sec", None, None),
            P("sec", None, None, None),
            P(),
            P("sec", "elem"),
            P("sec", "elem"),
            P("sec", "elem"),
        ),
        out_specs=P("sec", None, "elem"),
        check_vma=False,
    )
```

```python
import functools

import jax
import jax.numpy as jnp
from jax import lax
from jax.experimental import pallas as pl
from jax.experimental.pallas import tpu as pltpu
from jax.sharding import PartitionSpec as P

NODES = 64
HALO = 256
LANES = 128
ROWS = 4
DEPTH = 384
PARTS = DEPTH // LANES
STEP = 0.25
MESH = pl.DeviceIdType.MESH
F32 = jnp.float32
BF16 = jnp.bfloat16


def split(value):
    high = value.astype(BF16)
    return high, (value - high.astype(F32)).astype(BF16)


def kernel(
    n,
    links,
    scale,
    donors,
    select,
    fields,
    volume,
    faces,
    patterns,
    choose,
    out,
    table,
    landed,
    first,
    second,
    donated,
    outgoing,
    packed,
    rims,
    operand,
    weights,
    padded,
    own,
    mapped,
    block_send,
    block_recv,
    rim_send,
    rim_recv,
):
    sec, me = lax.axis_index("sec"), lax.axis_index("elem")
    other = 1 - sec
    elements = fields.shape[1]
    slots = donors.shape[1]
    per_device = slots // n
    block = per_device * ROWS
    components = fields.shape[0]
    tail = components - 2 * LANES

    barrier = pltpu.get_barrier_semaphore()
    for j in range(n):
        pl.semaphore_signal(barrier, inc=1, device_id=(other, j), device_id_type=MESH)

    @pl.when(me > 0)
    def _():
        pl.semaphore_signal(barrier, inc=1, device_id=(sec, me - 1), device_id_type=MESH)

    @pl.when(me < n - 1)
    def _():
        pl.semaphore_signal(barrier, inc=1, device_id=(sec, me + 1), device_id_type=MESH)

    for c in range(elements // LANES):
        for j in range(PARTS):
            if j < 2:
                piece = fields[j * LANES : (j + 1) * LANES, c * LANES : (c + 1) * LANES]
            else:
                piece = jnp.concatenate(
                    [
                        fields[2 * LANES : components, c * LANES : (c + 1) * LANES],
                        jnp.zeros((LANES - tail, LANES), F32),
                    ],
                    axis=0,
                )
            table[pl.ds(c * LANES * ROWS + j, LANES, stride=ROWS), :] = jnp.transpose(piece)
        table[pl.ds(c * LANES * ROWS + 3, LANES, stride=ROWS), :] = jnp.zeros((LANES, LANES), F32)

    def prepare_weights():
        padded[...] = jnp.zeros_like(padded)
        for f in range(7):
            padded[0:components, 0:components] = volume[...] if f == 6 else faces[f]
            for k in range(PARTS):
                strip = jnp.transpose(padded[:, k * LANES : (k + 1) * LANES])
                high, low = split(strip)
                pair, lanes = f // 2, slice(f % 2 * DEPTH, f % 2 * DEPTH + DEPTH)
                if k < 2:
                    places = ((k * LANES, high), ((2 + k) * LANES, high), ((4 + k) * LANES, low))
                    for row, value in places:
                        weights[pair, row : row + LANES, lanes] = value
                else:
                    ends = (high[:tail], high[:tail], low[:tail], jnp.zeros_like(low[:tail]))
                    for m, value in enumerate(ends):
                        row = 6 * LANES + m * tail
                        weights[pair, row : row + tail, lanes] = value

    def rim_copy(stage, side):
        target = me - 1 if side == 0 else me + 1
        return pltpu.make_async_remote_copy(
            src_ref=packed.at[side],
            dst_ref=rims.at[stage, 1 - side],
            send_sem=rim_send.at[stage, side],
            recv_sem=rim_recv.at[stage, 1 - side],
            device_id=(sec, target),
            device_id_type=MESH,
        )

    def to_operand(row, count, parts):
        rows = pl.ds(row, count)
        for k in range(2):
            high, low = split(parts[k])
            operand[rows, k * LANES : (k + 1) * LANES] = high
            operand[rows, (2 + k) * LANES : (3 + k) * LANES] = low
            operand[rows, (4 + k) * LANES : (5 + k) * LANES] = high
        high, low = split(parts[2])
        both = high.astype(F32) + pltpu.roll(low.astype(F32), tail, 1)
        operand[rows, 6 * LANES : 7 * LANES] = both.astype(BF16)
        operand[rows, 7 * LANES : 8 * LANES] = high

    def face_products(row):
        def body(pair, carry):
            y = jnp.dot(
                operand[pl.ds(pl.multiple_of(row, HALO), HALO), :],
                weights[pair],
                preferred_element_type=F32,
            )
            for half in range(2):
                for k in range(PARTS):
                    at = half * DEPTH + k * LANES
                    mapped[pair * 2 + half, pl.ds(row * ROWS + k, HALO, stride=ROWS), :] = y[:, at : at + LANES]
            return carry

        lax.fori_loop(0, 3, body, 0)

    for stage in range(2):
        state = first if stage == 0 else second

        def donate(i, carry):
            for u in range(8):
                b = i * 8 + u
                row = donors[0, b] * ROWS
                donated[pl.ds(pl.multiple_of(b * ROWS, ROWS), ROWS), :] = table[pl.ds(row, ROWS), :]
            return carry

        lax.fori_loop(0, slots // 8, donate, 0)
        values = donated[...]
        shape = (slots * ROWS, slots)
        mine = lax.broadcasted_iota(jnp.int32, shape, 0) // ROWS == lax.broadcasted_iota(jnp.int32, shape, 1)
        kinds = jnp.sum(jnp.where(mine, choose[...].astype(F32), 0.0), axis=1, keepdims=True)
        result = jnp.zeros((slots * ROWS, LANES), F32)
        for p in range(patterns.shape[0]):
            one = patterns[p]
            none = jnp.zeros_like(one)
            twice = jnp.concatenate(
                [jnp.concatenate([one, none], axis=1), jnp.concatenate([none, one], axis=1)], axis=0
            )
            moved = lax.dot_general(
                values,
                twice,
                (((1,), (1,)), ((), ())),
                precision=lax.Precision.HIGHEST,
                preferred_element_type=F32,
            )
            result = jnp.where(kinds == float(p), moved, result)
        outgoing[...] = result

        if stage == 0:
            heard = n + (me > 0).astype(jnp.int32) + (me < n - 1).astype(jnp.int32)
            pl.semaphore_wait(barrier, heard)

        def block_copy(j):
            return pltpu.make_async_remote_copy(
                src_ref=outgoing.at[pl.ds(pl.multiple_of(j * block, block), block)],
                dst_ref=landed.at[stage, pl.ds(pl.multiple_of(me * block, block), block)],
                send_sem=block_send.at[stage, j],
                recv_sem=block_recv.at[stage, me],
                device_id=(other, j),
                device_id_type=MESH,
            )

        def arrived(j):
            return pltpu.make_async_remote_copy(
                src_ref=outgoing.at[pl.ds(pl.multiple_of(j * block, block), block)],
                dst_ref=landed.at[stage, pl.ds(pl.multiple_of(j * block, block), block)],
                send_sem=block_send.at[stage, j],
                recv_sem=block_recv.at[stage, j],
                device_id=(other, j),
                device_id_type=MESH,
            )

        for j in range(n):
            block_copy(j).start()
        if stage == 0:
            prepare_weights()
        for j in range(n):
            arrived(j).wait_recv()
        table[elements * ROWS :, :] = landed[stage]

        def pick(i, carry):
            group = [table[pl.ds(select[0, i * 8 + u] * ROWS, ROWS), :] for u in range(8)]
            for u in range(8):
                state[pl.ds(pl.multiple_of((i * 8 + u) * ROWS, ROWS), ROWS), :] = group[u]
            return carry

        def rim_parts(row):
            return [state[pl.ds(row * ROWS + k, HALO, stride=ROWS), :] for k in range(PARTS)]

        for side, begin in ((0, 0), (1, elements - HALO)):
            lax.fori_loop(begin // 8, (begin + HALO) // 8, pick, 0)
            parts = rim_parts(begin)
            packed[side, 0:HALO, :] = parts[0]
            packed[side, HALO : 2 * HALO, :] = parts[1]
            lower, upper = parts[2][: HALO // 2], parts[2][HALO // 2 :]
            packed[side, 2 * HALO :, :] = lower + pltpu.roll(upper, tail, 1)

            @pl.when(me > 0 if side == 0 else me < n - 1)
            def _():
                rim_copy(stage, side).start()

            to_operand(HALO + begin, HALO, parts)
        lax.fori_loop(HALO // 8, (elements - HALO) // 8, pick, 0)
        for c in range(1, elements // HALO - 1):
            to_operand(HALO + c * HALO, HALO, rim_parts(c * HALO))

        def own_products(c, carry):
            row = HALO + c * HALO
            face_products(row)
            y = jnp.dot(
                operand[pl.ds(pl.multiple_of(row, HALO), HALO), :],
                weights[3, :, 0:DEPTH],
                preferred_element_type=F32,
            )
            for k in range(PARTS):
                own[pl.ds(c * HALO * ROWS + k, HALO, stride=ROWS), :] = y[:, k * LANES : (k + 1) * LANES]
            return carry

        lax.fori_loop(0, elements // HALO, own_products, 0)

        for side in (1, 0):
            row = 0 if side == 0 else HALO + elements
            inside = me > 0 if side == 0 else me < n - 1

            @pl.when(inside)
            def _():
                rim_copy(stage, 1 - side).wait_recv()
                folded = rims[stage, side, 2 * HALO :, :]
                lane = lax.broadcasted_iota(jnp.int32, folded.shape, 1)
                lower = jnp.where(lane < tail, folded, 0.0)
                upper = jnp.where(lane < tail, pltpu.roll(folded, LANES - tail, 1), 0.0)
                last = jnp.concatenate([lower, upper], axis=0)
                to_operand(row, HALO, [rims[stage, side, 0:HALO, :], rims[stage, side, HALO : 2 * HALO, :], last])
                face_products(row)

            @pl.when(jnp.logical_not(inside))
            def _():
                for f in range(6):
                    mapped[f, row * ROWS : (row + HALO) * ROWS, :] = jnp.zeros((HALO * ROWS, LANES), F32)

        def advance(i, carry):
            group = []
            for u in range(8):
                g = i * 8 + u
                here = pl.ds(pl.multiple_of(g * ROWS, ROWS), ROWS)
                pieces = [mapped[f, pl.ds(links[f, 0, g] * ROWS, ROWS), :] for f in range(6)]
                total = (pieces[0] + pieces[1]) + (pieces[2] + pieces[3]) + (pieces[4] + pieces[5])
                stepped = state[here, :] + scale[0, g] * (STEP * (own[here, :] + total))
                if stage == 1:
                    stepped = 0.5 * first[here, :] + 0.5 * stepped
                group.append((here, stepped))
            for here, stepped in group:
                table[here, :] = stepped
            return carry

        lax.fori_loop(0, elements // 8, advance, 0)
        for j in range(n):
            block_copy(j).wait_send()
        for side in range(2):

            @pl.when(me > 0 if side == 0 else me < n - 1)
            def _():
                rim_copy(stage, side).wait_send()

    for c in range(elements // LANES):
        for j in range(PARTS):
            piece = jnp.transpose(table[pl.ds(c * LANES * ROWS + j, LANES, stride=ROWS), :])
            high = min((j + 1) * LANES, components)
            out[j * LANES : high, c * LANES : (c + 1) * LANES] = piece[: high - j * LANES]


def local(
    n,
    fields,
    jacobian,
    face_links,
    volume_matrix,
    face_matrices,
    patterns,
    donor_index,
    pattern_index,
    receivers,
):
    components, elements = fields.shape[1:]
    slots = donor_index.shape[1]
    slot = jnp.arange(slots, dtype=jnp.int32)
    hit = receivers[0][None, :] == jnp.arange(elements, dtype=jnp.int32)[:, None]
    found = jnp.max(jnp.where(hit, slot[None, :], -1), axis=1)
    index = jnp.arange(elements, dtype=jnp.int32)
    select = jnp.where(found >= 0, elements + found, index)[None]
    smem = pl.BlockSpec(memory_space=pltpu.SMEM)
    vmem = pl.BlockSpec(memory_space=pltpu.VMEM)
    wide = elements + 2 * HALO
    result = pl.pallas_call(
        functools.partial(kernel, n),
        out_shape=jax.ShapeDtypeStruct((components, elements), F32),
        in_specs=[smem] * 4 + [vmem] * 5,
        out_specs=vmem,
        scratch_shapes=[
            pltpu.VMEM(((elements + slots) * ROWS, LANES), F32),
            pltpu.VMEM((2, slots * ROWS, LANES), F32),
            pltpu.VMEM((elements * ROWS, LANES), F32),
            pltpu.VMEM((elements * ROWS, LANES), F32),
            pltpu.VMEM((slots * ROWS, LANES), F32),
            pltpu.VMEM((slots * ROWS, LANES), F32),
            pltpu.VMEM((2, 5 * HALO // 2, LANES), F32),
            pltpu.VMEM((2, 2, 5 * HALO // 2, LANES), F32),
            pltpu.VMEM((wide, 8 * LANES), BF16),
            pltpu.VMEM((4, 8 * LANES, 2 * DEPTH), BF16),
            pltpu.VMEM((DEPTH, DEPTH), F32),
            pltpu.VMEM((elements * ROWS, LANES), F32),
            pltpu.VMEM((6, wide * ROWS, LANES), F32),
            pltpu.SemaphoreType.DMA((2, n)),
            pltpu.SemaphoreType.DMA((2, n)),
            pltpu.SemaphoreType.DMA((2, 2)),
            pltpu.SemaphoreType.DMA((2, 2)),
        ],
        compiler_params=pltpu.CompilerParams(
            collective_id=0, has_side_effects=True, vmem_limit_bytes=62 * 1024 * 1024
        ),
    )(
        jnp.transpose(face_links, (1, 0, 2)),
        jacobian,
        donor_index,
        select,
        fields[0],
        volume_matrix[0],
        face_matrices[0],
        patterns,
        pattern_index,
    )
    return result[None]


def solution(mesh):
    return jax.shard_map(
        functools.partial(local, mesh.shape["elem"]),
        mesh=mesh,
        in_specs=(
            P("sec", None, "elem"),
            P("sec", "elem"),
            P("sec", None, "elem"),
            P("sec", None, None),
            P("sec", None, None, None),
            P(),
            P("sec", "elem"),
            P("sec", "elem"),
            P("sec", "elem"),
        ),
        out_specs=P("sec", None, "elem"),
        check_vma=False,
    )
```
